32 devices in a mesh: groups: 2 (over x), out: 16 (over z, y, core).
Axes of the slice: x: 2, y: 2, z: 4, core: 2. Of those that a mesh axis runs over, the one named last changes fastest.
Arguments:
- tokens: bfloat16 [256, 8192], P('groups', 'out'), parts along dimension 0, may hold values from -60 to 60, as said below
- grad_hidden: bfloat16 [256, 16384], P('groups', 'out'), parts along dimension 0, may hold values from -6 to 6
- w_gate: bfloat16 [8192, 16384], P(None, 'out'), may hold values from -0.0625 to 0.0625
- w_up: bfloat16 [8192, 16384], P(None, 'out'), may hold values from -0.0625 to 0.0625
- a_factors: bfloat16 [8192, 128], replicated, may hold values from -0.0625 to 0.0625
- b_factors: bfloat16 [2, 64, 16384], P(None, None, 'out'), may hold values from -0.75 to 0.75
- magnitudes: float32 [2, 16384], P(None, 'out'), may hold values from 1 to 2
Outputs:
- hidden: bfloat16 [256, 16384], P('groups', 'out'), parts along dimension 0
- grad_tokens: bfloat16 [256, 8192], P('groups', 'out'), parts along dimension 0
- step_a: float32 [16384, 128], P(('groups', 'out')), parts along dimension 0
- step_b: float32 [4, 64, 16384], P('groups', None, 'out'), parts along dimension 0
- step_m: float32 [4, 16384], P('groups', 'out'), parts along dimension 0
The draws below stay inside these ranges and needn't reach their ends.
There are 2 independent parts, one for each index of `groups`. The reference program is written for one: setup_inputs(seed, part) draws one part's arguments, and reference() takes and returns one part's arrays. A program takes and returns all parts, laid end to end along the dimension named above; an argument that names none is the same for every part. Nothing has to cross between parts.
Inputs may be any that keep to these rules, and one draw needn't show every extreme that they name: `tokens`: activations with feature scales that differ between features.
All inputs are finite; a program needn't handle non-finite values.
Results may differ from the reference program's by a relative error of at most 0.0073.
Values may be sent and summed in bfloat16 or wider, within the bound.
A program may use at most 128 MiB of HBM per device.

```python
import jax
import jax.numpy as jnp
from jax import lax

D = 8192
FW = 16384
R = 64
TOKENS = 128


def draw_tokens(key, part):
    first_key = jax.random.fold_in(jax.random.fold_in(key, 11), 0)
    channel = 3.0 ** (jnp.arange(D, dtype=jnp.float32) / max(D - 1, 1))
    values = jnp.clip(jax.random.normal(first_key, (TOKENS, D), jnp.float32), -5.0, 5.0)
    return (values * channel[None, :]).astype(jnp.bfloat16)


def shard_levels(key, shape, cuts, smallest, high):
    def one(axis_at, blocks):
        steps = jax.random.uniform(jax.random.fold_in(jax.random.fold_in(key, 6), axis_at), (blocks,), jnp.float32, smallest / len(cuts), high / len(cuts))
        return jnp.repeat(jnp.exp(steps), shape[axis_at] // blocks).reshape((-1,) + (1,) * (len(shape) - axis_at - 1))

    factor_of = one(*cuts[0])
    for cut in cuts[1:]:
        factor_of = factor_of * one(*cut)
    return factor_of


def bell_draw(stream_key, dims, deviation, reach, pieces=(), kind=jnp.bfloat16):
    gain = shard_levels(stream_key, dims, pieces, -0.22, 0.18) if pieces else 1.0
    array = jax.random.normal(stream_key, dims, jnp.float32) * deviation * gain
    return jnp.minimum(jnp.maximum(array, -reach), reach).astype(kind)


def setup_inputs(seed: int = 0, part: int = 0) -> dict:
    splits = jax.random.split(jax.random.key(seed), 8)
    own_keys = jax.random.split(jax.random.fold_in(splits[7], part), 8)
    return {
        "tokens": draw_tokens(jax.random.fold_in(jax.random.fold_in(splits[7], part), 71), part),
        "grad_hidden": bell_draw(own_keys[1], (TOKENS, FW), 1.0, 6.0, ((1, 16),)),
        "w_gate": bell_draw(splits[2], (D, FW), D ** -0.5, 0.0625, ((1, 16),)),
        "w_up": bell_draw(splits[3], (D, FW), D ** -0.5, 0.0625, ((1, 16),)),
        "a_factors": bell_draw(splits[4], (D, 2 * R), D ** -0.5, 0.0625),
        "b_factors": bell_draw(splits[5], (2, R, FW), R ** -0.5, 0.75, ((2, 16),)),
        "magnitudes": jnp.clip(1.0 + 1.0 * jax.random.uniform(splits[6], (2, FW), jnp.float32) ** shard_levels(splits[6], (2, FW), ((1, 16),), -0.2, 0.2), 1.0, 2.0),
    }


def reference(tokens, grad_hidden, w_gate, w_up, a_factors, b_factors, magnitudes):
    weights = (w_gate, w_up)
    low = jnp.dot(tokens, a_factors, preferred_element_type=jnp.float32).astype(jnp.bfloat16)
    norms = []
    scales = []
    bases = []
    pres = []
    for which in range(2):
        left = a_factors[:, which * R:(which + 1) * R]
        right = b_factors[which]
        merged = weights[which].astype(jnp.float32) + jnp.dot(left, right, preferred_element_type=jnp.float32)
        norm_col = jnp.sqrt(lax.optimization_barrier(jnp.sum(merged * merged, axis=0)) + 1e-06)
        scale = magnitudes[which] / norm_col
        base = jnp.dot(tokens, weights[which], preferred_element_type=jnp.float32)
        base = base + jnp.dot(low[:, which * R:(which + 1) * R], right, preferred_element_type=jnp.float32)
        norms.append(norm_col)
        scales.append(scale)
        bases.append(base)
        pres.append(base * scale[None, :])
    sigma = jax.nn.sigmoid(pres[0])
    hidden = (pres[0] * sigma * pres[1]).astype(jnp.bfloat16)
    cotangent = grad_hidden.astype(jnp.float32)
    dpres = (cotangent * pres[1] * sigma * (1.0 + pres[0] * (1.0 - sigma)), cotangent * pres[0] * sigma)
    partial_sum = jnp.zeros((tokens.shape[0], tokens.shape[1]), jnp.float32)
    z_blocks = []
    grad_bs = []
    grad_ms = []
    for which in range(2):
        dscaled = (dpres[which] * scales[which][None, :]).astype(jnp.bfloat16)
        grad_ms.append(lax.optimization_barrier(jnp.sum(dpres[which] * bases[which], axis=0)) / norms[which])
        grad_bs.append(jnp.dot(low[:, which * R:(which + 1) * R].T, dscaled, preferred_element_type=jnp.float32))
        z_blocks.append(jnp.dot(dscaled, b_factors[which].T, preferred_element_type=jnp.float32))
        partial_sum = partial_sum + jnp.dot(dscaled, weights[which].T, preferred_element_type=jnp.float32)
    z_all = jnp.concatenate(z_blocks, axis=1)
    a_wide = a_factors.astype(jnp.float32)
    grad_tokens = (partial_sum + jnp.dot(z_all, a_wide.T, precision=lax.Precision.HIGHEST)).astype(jnp.bfloat16)
    grad_a = jnp.dot(tokens.astype(jnp.float32).T, z_all, precision=lax.Precision.HIGHEST)
    grad_b = jnp.stack(grad_bs)
    grad_m = jnp.stack(grad_ms)
    energy = jnp.sum(grad_a * grad_a) + jnp.sum(grad_b * grad_b) + jnp.sum(grad_m * grad_m)
    count_all = 2 * D * R + 2 * R * FW + 2 * FW
    rms_value = jnp.sqrt(energy / count_all + 1e-06)
    return (hidden, grad_tokens, grad_a / rms_value, grad_b / rms_value, grad_m / rms_value)
```

```python
import functools

import jax
import jax.numpy as jnp
from jax import lax
from jax.experimental import pallas as pl
from jax.experimental.pallas import tpu as pltpu
from jax.sharding import PartitionSpec as P

F32 = jnp.float32
BF16 = jnp.bfloat16
CHUNKS = 8
LANES = 8


def mm(left, right):
    return lax.dot_general(left, right, (((1,), (0,)), ((), ())), preferred_element_type=F32)


def mm_t(left, right):
    return lax.dot_general(left, right, (((1,), (1,)), ((), ())), preferred_element_type=F32)


def mm_tn(left, right):
    return lax.dot_general(left, right, (((0,), (0,)), ((), ())), preferred_element_type=F32)


def mm_full(left, right):
    return lax.dot_general(
        left, right, (((1,), (0,)), ((), ())),
        precision=lax.Precision.HIGHEST, preferred_element_type=F32,
    )


def split_parts(values):
    upper = values.astype(BF16)
    lower = (values - upper.astype(F32)).astype(BF16)
    return upper, lower


def fold_rows(values):
    rows, cols = values.shape
    return jnp.sum(values.reshape(rows // 8, 8, cols), axis=0)


def kernel(
    n, tok, gh, wg, wu, a, b, mag,
    hidden, gtok, step_a, step_b, step_m,
    wbuf, gat, ghv, bd, magv, sq, aw, base, gram, nrm, scl, ds, dt,
    hidv, gtv, sav, sbv, smv,
    qo, qs, qr, ys, yr, ps, pr, po, cs, cr, z0, zr, zs, zsum,
    w_sem, in_sem, out_sem, ga_send, ga_recv, q_sem, qr_sem, y_sem, yr_sem,
    p_sem, pr_sem, c_sem, cr_sem, z_sem, zr_sem,
):
    nh = n // 4
    tokens, block = tok.shape
    depth, cols = wg.shape
    wide = 2 * cols
    width = a.shape[1]
    rank = width // 2
    me = lax.axis_index("out")
    core = lax.rem(me, 2)
    mid = lax.rem(me // 2, 2)
    h = me // 4

    def place(hh, mm_, cc):
        return (hh * 2 + mm_) * 2 + cc

    core_peer = place(h, mid, 1 - core)
    mid_peer = place(h, 1 - mid, core)
    above = place(h + 1, mid, core)
    below = place(h - 1, mid, core)
    has_above = h < nh - 1
    has_below = h > 0
    at_end = jnp.logical_or(h == 0, h == nh - 1)
    inner = jnp.logical_and(h > 0, h < nh - 1)
    low_half = (h < nh // 2).astype(jnp.int32)
    mirrored = low_half * h + (1 - low_half) * (nh - 1 - h)

    def order(k):
        if k == 0:
            return h
        s = (k + 1) // 2
        near = mirrored - s if k % 2 else mirrored + s
        both = (2 * mirrored >= k).astype(jnp.int32)
        value = both * near + (1 - both) * k
        return low_half * value + (1 - low_half) * (nh - 1 - value)

    def remote(src, dst, send, recv, target):
        return pltpu.make_async_remote_copy(
            src_ref=src, dst_ref=dst, send_sem=send, recv_sem=recv,
            device_id={"out": target}, device_id_type=pl.DeviceIdType.MESH,
        )

    pending = []

    def start(copy, when=None):
        if when is None:
            copy.start()
        else:
            pl.when(when)(copy.start)
        pending.append((when, copy))

    own_load = pltpu.make_async_copy(tok, gat.at[me], in_sem.at[0])
    own_load.start()
    chunk = depth // CHUNKS

    def loads(j):
        rows = pl.ds(j * chunk, chunk)
        return (
            pltpu.make_async_copy(a.at[rows, :], wbuf.at[rows, pl.ds(wide, width)], w_sem.at[0, j]),
            pltpu.make_async_copy(wg.at[rows, :], wbuf.at[rows, pl.ds(0, cols)], w_sem.at[1, j]),
            pltpu.make_async_copy(wu.at[rows, :], wbuf.at[rows, pl.ds(cols, cols)], w_sem.at[2, j]),
        )

    small = (
        pltpu.make_async_copy(b.at[0], bd.at[pl.ds(0, rank), pl.ds(0, cols)], in_sem.at[1]),
        pltpu.make_async_copy(b.at[1], bd.at[pl.ds(rank, rank), pl.ds(cols, cols)], in_sem.at[2]),
        pltpu.make_async_copy(mag, magv, in_sem.at[3]),
        pltpu.make_async_copy(gh, ghv, in_sem.at[4]),
    )
    barrier = pltpu.get_barrier_semaphore()

    def greet(target):
        pl.semaphore_signal(
            barrier, inc=1, device_id={"out": target}, device_id_type=pl.DeviceIdType.MESH
        )

    pl.when(has_above)(lambda: greet(above))
    pl.when(has_below)(lambda: greet(below))
    greet(mid_peer)
    greet(core_peer)
    for j in range(CHUNKS):
        for copy in loads(j):
            copy.start()
    for copy in small:
        copy.start()
    bd[:rank, cols:] = jnp.zeros((rank, cols), BF16)
    bd[rank:, :cols] = jnp.zeros((rank, cols), BF16)
    own_load.wait()
    pl.semaphore_wait(barrier, 2 + has_above.astype(jnp.int32) + has_below.astype(jnp.int32))

    half = tokens // 2
    count = [0]

    def piece(origin, p):
        return gat.at[origin, pl.ds(p * half, half), :]

    def ga_out(origin, p, target, when=None):
        slot = count[0]
        count[0] += 1
        start(
            remote(piece(origin, p), piece(origin, p), ga_send.at[slot], ga_recv.at[origin, p], target),
            when,
        )

    def ga_wait(origin, p):
        remote(
            piece(origin, p), piece(origin, p), ga_send.at[0], ga_recv.at[origin, p], core_peer
        ).wait_recv()

    for p in range(2):
        ga_out(me, p, above, has_above)
        ga_out(me, p, below, has_below)
        ga_out(me, p, mid_peer)
    for p in range(2):
        ga_out(me, p, core_peer)

    def line(s, up, p):
        there = h - s if up else h + s
        exists = h >= s if up else h + s < nh
        origin = place(there, mid, core)
        pl.when(exists)(lambda: ga_wait(origin, p))
        go_on = has_above if up else has_below
        ga_out(origin, p, above if up else below, jnp.logical_and(exists, go_on))
        if not (s == 1 and p == 1):
            ga_out(origin, p, mid_peer, exists)
        ga_out(origin, p, core_peer, exists)

    def across(s, up, p):
        there = h - s if up else h + s
        exists = h >= s if up else h + s < nh
        origin = place(there, 1 - mid, core)
        pl.when(exists)(lambda: ga_wait(origin, p))
        ga_out(origin, p, core_peer, exists)

    def across_own(p):
        ga_wait(mid_peer, p)
        if p == 1:
            ga_out(mid_peer, p, above, has_above)
            ga_out(mid_peer, p, below, has_below)
        ga_out(mid_peer, p, core_peer)

    slots = {}
    for p in range(2):
        slots.setdefault(2 + p, []).append(functools.partial(across_own, p))
        for s in range(1, nh):
            for up in (True, False):
                slots.setdefault(2 * s + p, []).insert(0, functools.partial(line, s, up, p))
                slots.setdefault(2 * s + 2 + p, []).append(functools.partial(across, s, up, p))

    def norm_step(j):
        for copy in loads(j):
            copy.wait()
        rows = pl.ds(j * chunk, chunk)
        product = mm_tn(wbuf[rows, wide:], wbuf[rows, :])
        part = min(128, chunk)
        folded = jnp.zeros((8, wide), F32)
        for i in range(chunk // part):
            w = wbuf[pl.ds(j * chunk + i * part, part), :wide].astype(F32)
            folded += fold_rows(w * w)
        if j == 0:
            aw[...] = product
            sq[...] = folded
        else:
            aw[...] += product
            sq[...] += folded

    piece_cols = min(256, cols)

    def norm_end():
        for copy in small:
            copy.wait()
        g = aw[:, wide:]
        g_upper, rest = g.astype(BF16), g
        rest = rest - g_upper.astype(F32)
        g_middle = rest.astype(BF16)
        g_lower = (rest - g_middle.astype(F32)).astype(BF16)
        for c0 in range(0, wide, piece_cols):
            cut = slice(c0, c0 + piece_cols)
            right = bd[:, cut]
            gb = mm(g_upper, right) + (mm(g_middle, right) + mm(g_lower, right))
            cross = right.astype(F32) * (2.0 * aw[:, cut] + gb)
            square = jnp.sum(sq[:, cut], axis=0, keepdims=True) + jnp.sum(cross, axis=0, keepdims=True)
            norm = jnp.sqrt(jnp.maximum(square, 0.0) + 1e-06)
            which, off = c0 // cols, c0 % cols
            nrm[:, cut] = norm
            scl[:, cut] = magv[which : which + 1, off : off + piece_cols] / norm

    def forward(rows, x, first=False):
        product = mm(x, wbuf[rows, :])
        square = mm_t(x, x)
        if first:
            base[...] = product
            gram[...] = square
        else:
            base[...] += product
            gram[...] += square

    def quad(k, first=False):
        there = order(k)
        for m in range(2):
            for p in range(2):
                arrived(k, m, p)
        rows = pl.ds(pl.multiple_of(there * 4 * block, 4 * block), 4 * block)
        x = jnp.concatenate([gat[there * 4 + q] for q in range(4)], axis=1)
        forward(rows, x, first)

    def pair(k, other):
        for p in range(2):
            arrived(k, other, p)
        chip = order(k) * 2 + (1 - mid if other else mid)
        rows = pl.ds(pl.multiple_of(chip * 2 * block, 2 * block), 2 * block)
        x = jnp.concatenate([gat[chip * 2 + q] for q in range(2)], axis=1)
        forward(rows, x)

    def arrived(k, other, p):
        ga_wait(place(order(k), 1 - mid if other else mid, 1 - core), p)

    last_slot = max(slots)
    work = {}
    for j in range(CHUNKS):
        work.setdefault(min(1 + j // 2, 4), []).append(functools.partial(norm_step, j))
    work.setdefault(4, []).append(norm_end)
    work.setdefault(4, []).append(functools.partial(quad, 0, True))
    for k in range(1, nh - 1):
        work.setdefault(2 * k + 4, []).append(functools.partial(quad, k))
    work.setdefault(last_slot - 1, []).append(functools.partial(pair, nh - 1, 0))
    for slot in range(1, last_slot + 1):
        for event in slots.get(slot, []):
            event()
        for unit in work.get(slot, []):
            unit()
    pair(nh - 1, 1)

    outs = []

    def put(src, dst):
        copy = pltpu.make_async_copy(src, dst, out_sem.at[len(outs)])
        copy.start()
        outs.append(copy)

    low = base[:, wide:]
    low_bf = low.astype(BF16)
    for c0 in range(0, cols, piece_cols):
        cuts = (slice(c0, c0 + piece_cols), slice(cols + c0, cols + c0 + piece_cols))
        out_cut = slice(c0, c0 + piece_cols)
        bases = [base[:, cut] + mm(low_bf, bd[:, cut]) for cut in cuts]
        pres = [bases[q] * scl[:, cuts[q]] for q in range(2)]
        sigma = 1.0 / (1.0 + jnp.exp(-pres[0]))
        hidv[:, out_cut] = (pres[0] * sigma * pres[1]).astype(BF16)
        cot = ghv[:, out_cut].astype(F32)
        dpres = (
            cot * pres[1] * sigma * (1.0 + pres[0] * (1.0 - sigma)),
            cot * pres[0] * sigma,
        )
        for which in range(2):
            dscaled = (dpres[which] * scl[:, cuts[which]]).astype(BF16)
            ds[:, cuts[which]] = dscaled
            dt[cuts[which], :] = jnp.transpose(dscaled)
            smv[which : which + 1, out_cut] = (
                jnp.sum(dpres[which] * bases[which], axis=0, keepdims=True) / nrm[:, cuts[which]]
            )
    put(hidv, hidden)

    fine = block // 2

    def rows_at(p):
        return pl.ds(p * fine, fine)

    def partial(hh, m_, c_):
        rows = pl.ds(pl.multiple_of(place(hh, m_, c_) * block, block), block)
        return mm(wbuf[rows, :wide], dt[...])

    def dest(k):
        return order(nh - 1 - k)

    def q_first(k):
        qs[k] = partial(dest(k), 1 - mid, 1 - core).astype(BF16)
        for p in range(2):
            start(
                remote(
                    qs.at[k, rows_at(p), :], qr.at[k, rows_at(p), :],
                    q_sem.at[k, p], qr_sem.at[k, p], core_peer,
                )
            )
        qo[...] = partial(dest(k), 1 - mid, core)

    def q_second(k):
        for p in range(2):
            copy = remote(
                ys.at[k, rows_at(p), :], yr.at[k, rows_at(p), :],
                y_sem.at[k, p], yr_sem.at[k, p], mid_peer,
            )
            remote(
                qs.at[k, rows_at(p), :], qr.at[k, rows_at(p), :],
                q_sem.at[k, p], qr_sem.at[k, p], core_peer,
            ).wait_recv()
            ys[k, rows_at(p), :] = (qo[rows_at(p), :] + qr[k, rows_at(p), :].astype(F32)).astype(BF16)
            start(copy)

    def p_first(k):
        ps[k] = partial(dest(k), mid, 1 - core).astype(BF16)
        start(remote(ps.at[k], pr.at[k], p_sem.at[k], pr_sem.at[k], core_peer))
        po[k] = partial(dest(k), mid, core)

    def p_second(k):
        remote(ps.at[k], pr.at[k], p_sem.at[k], pr_sem.at[k], core_peer).wait_recv()
        po[k] = po[k] + pr[k].astype(F32)

    def y_wait(k, p):
        remote(
            ys.at[k, rows_at(p), :], yr.at[k, rows_at(p), :],
            y_sem.at[k, p], yr_sem.at[k, p], mid_peer,
        ).wait_recv()

    def chain_copy(k, p):
        there = dest(k)
        down = (there < h).astype(jnp.int32)
        return remote(
            cs.at[k, rows_at(p), :], cr.at[down, there, rows_at(p), :],
            c_sem.at[k, p], cr_sem.at[down, there, p],
            place(h + 1 - 2 * down, mid, core),
        )

    def chain_wait(down, there, p):
        remote(
            cs.at[0, rows_at(p), :], cr.at[down, there, rows_at(p), :],
            c_sem.at[0, p], cr_sem.at[down, there, p], core_peer,
        ).wait_recv()

    def chain(k, inside):
        @pl.when(inner if inside else at_end)
        def _():
            there = dest(k)
            down = (there < h).astype(jnp.int32)
            for p in range(2):
                y_wait(k, p)
                total = po[k, rows_at(p), :] + yr[k, rows_at(p), :].astype(F32)
                if inside:
                    chain_wait(down, there, p)
                    total += cr[down, there, rows_at(p), :].astype(F32)
                cs[k, rows_at(p), :] = total.astype(BF16)
                chain_copy(k, p).start()

    zrows = rank + LANES
    steps = [core_peer, mid_peer]
    flip = 1
    while flip < nh:
        bit = lax.rem(h // flip, 2)
        steps.append(place(h + flip * (1 - 2 * bit), mid, core))
        flip *= 2

    def z_copy(i):
        if i == 0:
            src, dst = z0.at[1 - core], zr.at[0]
        elif i == len(steps):
            src, dst = zsum.at[core], zsum.at[core]
        else:
            src, dst = zs.at[i], zr.at[i]
        target = core_peer if i == len(steps) else steps[i]
        return remote(src, dst, z_sem.at[i], zr_sem.at[i], target)

    def z_begin():
        low_t = jnp.transpose(low).astype(BF16)
        lanes = jnp.zeros((LANES, width), F32)
        first_row = lax.broadcasted_iota(jnp.int32, (LANES, width), 0) == 0
        for which in range(2):
            for c0 in range(0, cols, piece_cols):
                value = mm(
                    low_t[which * rank : (which + 1) * rank, :],
                    ds[:, which * cols + c0 : which * cols + c0 + piece_cols],
                )
                sbv[which, :, c0 : c0 + piece_cols] = value
                folded = fold_rows(value * value)
                for c1 in range(0, piece_cols, width):
                    lanes += folded[:, c1 : c1 + width]
                    row = smv[which : which + 1, c0 + c1 : c0 + c1 + width]
                    lanes += jnp.where(first_row, row * row, 0.0)
        z_t = mm(bd[...], dt[...])
        z0[0, :rank, :] = z_t[:rank]
        z0[1, :rank, :] = z_t[rank:]
        z0[0, rank:, :] = lanes
        z0[1, rank:, :] = jnp.zeros((LANES, width), F32)
        start(z_copy(0))

    def z_step(i):
        z_copy(i).wait_recv()
        total = (z0[core] if i == 0 else zs[i]) + zr[i]
        if i + 1 < len(steps):
            zs[i + 1] = total
        else:
            zsum[core] = total
        start(z_copy(i + 1))

    def tail():
        i = len(steps)
        remote(
            zsum.at[1 - core], zsum.at[1 - core], z_sem.at[i], zr_sem.at[i], core_peer
        ).wait_recv()
        z_t = jnp.concatenate([zsum[0, :rank, :], zsum[1, :rank, :]], axis=0)
        energies = jnp.sum(z_t * mm_full(z_t, gram[...]), axis=0, keepdims=True)
        energies += jnp.sum(zsum[0, rank:, :] + zsum[1, rank:, :], axis=0, keepdims=True)
        energy = jnp.sum(energies, axis=1, keepdims=True)
        entries = depth * width + 2 * rank * cols * n + 2 * cols * n
        inverse = 1.0 / jnp.sqrt(jnp.maximum(energy, 0.0) / entries + 1e-06)
        for which in range(2):
            sbv[which] = sbv[which] * inverse
        smv[...] = smv[...] * inverse
        put(sbv, step_b)
        put(smv, step_m)
        t_upper, t_lower = split_parts(z_t)
        mine = gat[me]
        sav[...] = jnp.transpose((mm(t_upper, mine) + mm(t_lower, mine)) * inverse)
        put(sav, step_a)
        a_mine = wbuf[pl.ds(pl.multiple_of(me * block, block), block), wide:]
        po[nh - 1] = po[nh - 1] + (mm(a_mine, t_upper) + mm(a_mine, t_lower))

    z_at = 0
    for k in range(nh):
        q_first(k)
        if k == 0:
            z_begin()
        q_second(k)
        if k > 0:
            p_second(k - 1)
        p_first(k)
        if z_at < len(steps):
            z_step(z_at)
            z_at += 1
        if 1 <= k < nh - 1:
            chain(k - 1, False)
        if k == nh - 2:
            chain(0, True)
    p_second(nh - 1)
    while z_at < len(steps):
        z_step(z_at)
        z_at += 1
    for k in range(nh - 2, nh - 1):
        chain(k, False)
    for k in range(1, nh - 1):
        chain(k, True)
    tail()
    for p in range(2):
        y_wait(nh - 1, p)
        po[nh - 1, rows_at(p), :] += yr[nh - 1, rows_at(p), :].astype(F32)
        for down, exists in ((0, has_below), (1, has_above)):

            @pl.when(exists)
            def _():
                chain_wait(down, h, p)
                po[nh - 1, rows_at(p), :] += cr[down, h, rows_at(p), :].astype(F32)

        gtv[:, p * fine : (p + 1) * fine] = jnp.transpose(po[nh - 1, rows_at(p), :]).astype(BF16)
    put(gtv, gtok)
    for k in range(nh - 1):
        for p in range(2):
            chain_copy(k, p).wait_send()
    for when, copy in pending:
        if when is None:
            copy.wait_send()
        else:
            pl.when(when)(copy.wait_send)
    for copy in outs:
        copy.wait()


def hand_on(*refs):
    for source, target in zip(refs[:5], refs[5:]):
        target[...] = source[...]


def per_device(n, tokens, grad_hidden, w_gate, w_up, a_factors, b_factors, magnitudes):
    count, block = tokens.shape
    depth, cols = w_gate.shape
    width = a_factors.shape[1]
    rank = width // 2
    nh = n // 4
    vmem = pl.BlockSpec(memory_space=pltpu.VMEM)
    hbm = pl.BlockSpec(memory_space=pl.ANY)
    dma = pltpu.SemaphoreType.DMA
    outs = (
        jax.ShapeDtypeStruct((count, cols), BF16),
        jax.ShapeDtypeStruct((count, block), BF16),
        jax.ShapeDtypeStruct((block, width), F32),
        jax.ShapeDtypeStruct((2, rank, cols), F32),
        jax.ShapeDtypeStruct((2, cols), F32),
    )
    z_steps = 2 + (nh - 1).bit_length()
    blocks = pltpu.VMEM((nh, block, count), BF16)
    z_half = (rank + LANES, count)
    results = pl.pallas_call(
        functools.partial(kernel, n),
        out_shape=outs,
        in_specs=[hbm] * 7,
        out_specs=(hbm,) * 5,
        scratch_shapes=[
            pltpu.VMEM((depth, 2 * cols + width), BF16),
            pltpu.VMEM((n, count, block), BF16),
            pltpu.VMEM((count, cols), BF16),
            pltpu.VMEM((width, 2 * cols), BF16),
            pltpu.VMEM((2, cols), F32),
            pltpu.VMEM((8, 2 * cols), F32),
            pltpu.VMEM((width, 2 * cols + width), F32),
            pltpu.VMEM((count, 2 * cols + width), F32),
            pltpu.VMEM((count, count), F32),
            pltpu.VMEM((1, 2 * cols), F32),
            pltpu.VMEM((1, 2 * cols), F32),
            pltpu.VMEM((count, 2 * cols), BF16),
            pltpu.VMEM((2 * cols, count), BF16),
        ]
        + [pltpu.VMEM(o.shape, o.dtype) for o in outs]
        + [
            pltpu.VMEM((block, count), F32),
            blocks, blocks, blocks, blocks, blocks, blocks,
            pltpu.VMEM((nh, block, count), F32),
            blocks,
            pltpu.VMEM((2, nh, block, count), BF16),
            pltpu.VMEM((2,) + z_half, F32),
            pltpu.VMEM((z_steps,) + z_half, F32),
            pltpu.VMEM((z_steps,) + z_half, F32),
            pltpu.VMEM((2,) + z_half, F32),
            dma((3, CHUNKS)),
            dma((5,)),
            dma((5,)),
            dma((20 * nh,)),
            dma((n, 2)),
            dma((nh, 2)),
            dma((nh, 2)),
            dma((nh, 2)),
            dma((nh, 2)),
            dma((nh,)),
            dma((nh,)),
            dma((nh, 2)),
            dma((2, nh, 2)),
            dma((z_steps + 1,)),
            dma((z_steps + 1,)),
        ],
        compiler_params=pltpu.CompilerParams(
            collective_id=0, has_side_effects=True, vmem_limit_bytes=60 * 1024 * 1024
        ),
    )(tokens, grad_hidden, w_gate, w_up, a_factors, b_factors, magnitudes)
    return pl.pallas_call(
        hand_on,
        out_shape=tuple(jax.ShapeDtypeStruct(r.shape, r.dtype) for r in results),
        in_specs=[vmem] * 5,
        out_specs=(vmem,) * 5,
    )(*results)


def solution(mesh):
    in_specs = (
        P("groups", "out"),
        P("groups", "out"),
        P(None, "out"),
        P(None, "out"),
        P(),
        P(None, None, "out"),
        P(None, "out"),
    )
    out_specs = (
        P("groups", "out"),
        P("groups", "out"),
        P(("groups", "out"), None),
        P("groups", None, "out"),
        P("groups", "out"),
    )
    return jax.shard_map(
        functools.partial(per_device, mesh.shape["out"]),
        mesh=mesh, in_specs=in_specs, out_specs=out_specs, check_vma=False,
    )
```

```python
import functools

import jax
import jax.numpy as jnp
from jax import lax
from jax.experimental import pallas as pl
from jax.experimental.pallas import tpu as pltpu
from jax.sharding import PartitionSpec as P

F32 = jnp.float32
BF16 = jnp.bfloat16
CHUNKS = 8
LANES = 8
PARTS = 2


def mm(left, right):
    return lax.dot_general(left, right, (((1,), (0,)), ((), ())), preferred_element_type=F32)


def mm_t(left, right):
    return lax.dot_general(left, right, (((1,), (1,)), ((), ())), preferred_element_type=F32)


def mm_tn(left, right):
    return lax.dot_general(left, right, (((0,), (0,)), ((), ())), preferred_element_type=F32)


def mm_full(left, right):
    return lax.dot_general(
        left, right, (((1,), (0,)), ((), ())),
        precision=lax.Precision.HIGHEST, preferred_element_type=F32,
    )


def split_parts(values):
    upper = values.astype(BF16)
    lower = (values - upper.astype(F32)).astype(BF16)
    return upper, lower


def fold_rows(values):
    rows, cols = values.shape
    return jnp.sum(values.reshape(rows // 8, 8, cols), axis=0)


def kernel(
    n, tok, gh, wg, wu, a, b, mag,
    hidden, gtok, step_a, step_b, step_m,
    wbuf, gat, ghv, bd, magv, sq, aw, base, gram, nrm, scl, ds, dt,
    hidv, gtv, sav, sbv, smv,
    qo, qs, qr, ys, yr, ps, pr, po, cs, cr, z0, zr, zs, zsum, zl,
    w_sem, in_sem, out_sem, ga_send, ga_recv, q_sem, qr_sem, y_sem, yr_sem,
    p_sem, pr_sem, c_sem, cr_sem, z_sem, zr_sem,
):
    nh = n // 4
    tokens, block = tok.shape
    depth, cols = wg.shape
    wide = 2 * cols
    width = a.shape[1]
    rank = width // 2
    me = lax.axis_index("out")
    core = lax.rem(me, 2)
    mid = lax.rem(me // 2, 2)
    h = me // 4

    def place(hh, mm_, cc):
        return (hh * 2 + mm_) * 2 + cc

    core_peer = place(h, mid, 1 - core)
    mid_peer = place(h, 1 - mid, core)
    above = place(h + 1, mid, core)
    below = place(h - 1, mid, core)
    has_above = h < nh - 1
    has_below = h > 0
    at_end = jnp.logical_or(h == 0, h == nh - 1)
    inner = jnp.logical_and(h > 0, h < nh - 1)
    low_half = (h < nh // 2).astype(jnp.int32)
    mirrored = low_half * h + (1 - low_half) * (nh - 1 - h)

    def order(k):
        if k == 0:
            return h
        s = (k + 1) // 2
        near = mirrored - s if k % 2 else mirrored + s
        both = (2 * mirrored >= k).astype(jnp.int32)
        value = both * near + (1 - both) * k
        return low_half * value + (1 - low_half) * (nh - 1 - value)

    def dest(k):
        if k == nh - 1:
            return h
        early = (mirrored > k).astype(jnp.int32)
        value = early * k + (1 - early) * (nh - 1 - k + mirrored)
        return low_half * value + (1 - low_half) * (nh - 1 - value)

    def remote(src, dst, send, recv, target):
        return pltpu.make_async_remote_copy(
            src_ref=src, dst_ref=dst, send_sem=send, recv_sem=recv,
            device_id={"out": target}, device_id_type=pl.DeviceIdType.MESH,
        )

    pending = []

    def start(copy, when=None):
        if when is None:
            copy.start()
        else:
            pl.when(when)(copy.start)
        pending.append((when, copy))

    own_load = pltpu.make_async_copy(tok, gat.at[me], in_sem.at[0])
    own_load.start()
    chunk = depth // CHUNKS

    def loads(j):
        rows = pl.ds(j * chunk, chunk)
        return (
            pltpu.make_async_copy(a.at[rows, :], wbuf.at[rows, pl.ds(wide, width)], w_sem.at[0, j]),
            pltpu.make_async_copy(wg.at[rows, :], wbuf.at[rows, pl.ds(0, cols)], w_sem.at[1, j]),
            pltpu.make_async_copy(wu.at[rows, :], wbuf.at[rows, pl.ds(cols, cols)], w_sem.at[2, j]),
        )

    small = (
        pltpu.make_async_copy(b.at[0], bd.at[pl.ds(0, rank), pl.ds(0, cols)], in_sem.at[1]),
        pltpu.make_async_copy(b.at[1], bd.at[pl.ds(rank, rank), pl.ds(cols, cols)], in_sem.at[2]),
        pltpu.make_async_copy(mag, magv, in_sem.at[3]),
        pltpu.make_async_copy(gh, ghv, in_sem.at[4]),
    )
    barrier = pltpu.get_barrier_semaphore()

    def greet(target):
        pl.semaphore_signal(
            barrier, inc=1, device_id={"out": target}, device_id_type=pl.DeviceIdType.MESH
        )

    pl.when(has_above)(lambda: greet(above))
    pl.when(has_below)(lambda: greet(below))
    greet(mid_peer)
    greet(core_peer)
    for j in range(CHUNKS):
        for copy in loads(j):
            copy.start()
    for copy in small:
        copy.start()
    bd[:rank, cols:] = jnp.zeros((rank, cols), BF16)
    bd[rank:, :cols] = jnp.zeros((rank, cols), BF16)
    own_load.wait()
    pl.semaphore_wait(barrier, 2 + has_above.astype(jnp.int32) + has_below.astype(jnp.int32))

    half = tokens // 2
    count = [0]

    def piece(origin, p):
        return gat.at[origin, pl.ds(p * half, half), :]

    def ga_out(origin, p, target, when=None):
        slot = count[0]
        count[0] += 1
        start(
            remote(piece(origin, p), piece(origin, p), ga_send.at[slot], ga_recv.at[origin, p], target),
            when,
        )

    def ga_wait(origin, p):
        remote(
            piece(origin, p), piece(origin, p), ga_send.at[0], ga_recv.at[origin, p], core_peer
        ).wait_recv()

    for p in range(2):
        ga_out(me, p, above, has_above)
        ga_out(me, p, below, has_below)
        ga_out(me, p, mid_peer)
    for p in range(2):
        ga_out(me, p, core_peer)

    def line(s, up, p):
        there = h - s if up else h + s
        exists = h >= s if up else h + s < nh
        origin = place(there, mid, core)
        pl.when(exists)(lambda: ga_wait(origin, p))
        go_on = has_above if up else has_below
        ga_out(origin, p, above if up else below, jnp.logical_and(exists, go_on))
        if not (s == 1 and p == 1):
            ga_out(origin, p, mid_peer, exists)
        ga_out(origin, p, core_peer, exists)

    def across(s, up, p):
        there = h - s if up else h + s
        exists = h >= s if up else h + s < nh
        origin = place(there, 1 - mid, core)
        pl.when(exists)(lambda: ga_wait(origin, p))
        ga_out(origin, p, core_peer, exists)

    def across_own(p):
        ga_wait(mid_peer, p)
        if p == 1:
            ga_out(mid_peer, p, above, has_above)
            ga_out(mid_peer, p, below, has_below)
        ga_out(mid_peer, p, core_peer)

    slots = {}
    for p in range(2):
        slots.setdefault(2 + p, []).append(functools.partial(across_own, p))
        for s in range(1, nh):
            for up in (True, False):
                slots.setdefault(2 * s + p, []).insert(0, functools.partial(line, s, up, p))
                slots.setdefault(2 * s + 2 + p, []).append(functools.partial(across, s, up, p))

    def norm_step(j):
        for copy in loads(j):
            copy.wait()
        rows = pl.ds(j * chunk, chunk)
        product = mm_tn(wbuf[rows, wide:], wbuf[rows, :])
        part = min(128, chunk)
        folded = jnp.zeros((8, wide), F32)
        for i in range(chunk // part):
            w = wbuf[pl.ds(j * chunk + i * part, part), :wide].astype(F32)
            folded += fold_rows(w * w)
        if j == 0:
            aw[...] = product
            sq[...] = folded
        else:
            aw[...] += product
            sq[...] += folded

    piece_cols = min(256, cols)

    def norm_end():
        for copy in small:
            copy.wait()
        g = aw[:, wide:]
        g_upper, rest = g.astype(BF16), g
        rest = rest - g_upper.astype(F32)
        g_middle = rest.astype(BF16)
        g_lower = (rest - g_middle.astype(F32)).astype(BF16)
        for c0 in range(0, wide, piece_cols):
            cut = slice(c0, c0 + piece_cols)
            right = bd[:, cut]
            gb = mm(g_upper, right) + (mm(g_middle, right) + mm(g_lower, right))
            cross = right.astype(F32) * (2.0 * aw[:, cut] + gb)
            square = jnp.sum(sq[:, cut], axis=0, keepdims=True) + jnp.sum(cross, axis=0, keepdims=True)
            norm = jnp.sqrt(jnp.maximum(square, 0.0) + 1e-06)
            which, off = c0 // cols, c0 % cols
            nrm[:, cut] = norm
            scl[:, cut] = magv[which : which + 1, off : off + piece_cols] / norm

    def forward(rows, x, first=False):
        product = mm(x, wbuf[rows, :])
        square = mm_t(x, x)
        if first:
            base[...] = product
            gram[...] = square
        else:
            base[...] += product
            gram[...] += square

    def quad(k, first=False):
        there = order(k)
        for m in range(2):
            for p in range(2):
                arrived(k, m, p)
        rows = pl.ds(pl.multiple_of(there * 4 * block, 4 * block), 4 * block)
        x = jnp.concatenate([gat[there * 4 + q] for q in range(4)], axis=1)
        forward(rows, x, first)

    def pair(k, other):
        for p in range(2):
            arrived(k, other, p)
        chip = order(k) * 2 + (1 - mid if other else mid)
        rows = pl.ds(pl.multiple_of(chip * 2 * block, 2 * block), 2 * block)
        x = jnp.concatenate([gat[chip * 2 + q] for q in range(2)], axis=1)
        forward(rows, x)

    def arrived(k, other, p):
        ga_wait(place(order(k), 1 - mid if other else mid, 1 - core), p)

    last_slot = max(slots)
    work = {}
    for j in range(CHUNKS):
        work.setdefault(min(1 + j // 2, 4), []).append(functools.partial(norm_step, j))
    work.setdefault(4, []).append(norm_end)
    work.setdefault(4, []).append(functools.partial(quad, 0, True))
    for k in range(1, nh - 1):
        work.setdefault(2 * k + 4, []).append(functools.partial(quad, k))
    work.setdefault(last_slot - 1, []).append(functools.partial(pair, nh - 1, 0))
    for slot in range(1, last_slot + 1):
        for event in slots.get(slot, []):
            event()
        for unit in work.get(slot, []):
            unit()
    pair(nh - 1, 1)

    outs = []

    def put(src, dst):
        copy = pltpu.make_async_copy(src, dst, out_sem.at[len(outs)])
        copy.start()
        outs.append(copy)

    low = base[:, wide:]
    low_bf = low.astype(BF16)
    for c0 in range(0, cols, piece_cols):
        cuts = (slice(c0, c0 + piece_cols), slice(cols + c0, cols + c0 + piece_cols))
        out_cut = slice(c0, c0 + piece_cols)
        bases = [base[:, cut] + mm(low_bf, bd[:, cut]) for cut in cuts]
        pres = [bases[q] * scl[:, cuts[q]] for q in range(2)]
        sigma = 1.0 / (1.0 + jnp.exp(-pres[0]))
        hidv[:, out_cut] = (pres[0] * sigma * pres[1]).astype(BF16)
        cot = ghv[:, out_cut].astype(F32)
        dpres = (
            cot * pres[1] * sigma * (1.0 + pres[0] * (1.0 - sigma)),
            cot * pres[0] * sigma,
        )
        for which in range(2):
            dscaled = (dpres[which] * scl[:, cuts[which]]).astype(BF16)
            ds[:, cuts[which]] = dscaled
            dt[cuts[which], :] = jnp.transpose(dscaled)
            smv[which : which + 1, out_cut] = (
                jnp.sum(dpres[which] * bases[which], axis=0, keepdims=True) / nrm[:, cuts[which]]
            )
    put(hidv, hidden)

    fine = block // PARTS

    def rows_at(p):
        return pl.ds(p * fine, fine)

    def partial(hh, m_, c_):
        rows = pl.ds(pl.multiple_of(place(hh, m_, c_) * block, block), block)
        return mm(wbuf[rows, :wide], dt[...])

    def q_copy(k, p):
        return remote(
            qs.at[k, rows_at(p), :], qr.at[k, rows_at(p), :],
            q_sem.at[k, p], qr_sem.at[k, p], core_peer,
        )

    def y_copy(k, p):
        return remote(
            ys.at[k, rows_at(p), :], yr.at[k, rows_at(p), :],
            y_sem.at[k, p], yr_sem.at[k, p], mid_peer,
        )

    def q_other(k):
        qs[k] = partial(dest(k), 1 - mid, 1 - core).astype(BF16)
        for p in range(PARTS):
            start(q_copy(k, p))

    def q_own(k):
        qo[...] = partial(dest(k), 1 - mid, core)

    def q_second(k):
        for p in range(PARTS):
            q_copy(k, p).wait_recv()
            ys[k, rows_at(p), :] = (qo[rows_at(p), :] + qr[k, rows_at(p), :].astype(F32)).astype(BF16)
            start(y_copy(k, p))

    def p_other(k):
        ps[k] = partial(dest(k), mid, 1 - core).astype(BF16)
        start(remote(ps.at[k], pr.at[k], p_sem.at[k], pr_sem.at[k], core_peer))

    def p_own(k):
        po[k] = partial(dest(k), mid, core)

    def p_second(k):
        remote(ps.at[k], pr.at[k], p_sem.at[k], pr_sem.at[k], core_peer).wait_recv()
        po[k] = po[k] + pr[k].astype(F32)

    ends = at_end.astype(jnp.int32)
    beside = low_half + (1 - low_half) * (nh - 2)
    end_place = (1 - low_half) * (nh - 1)

    def line_copy(k, p):
        there = dest(k)
        return remote(
            cs.at[k, rows_at(p), :], cr.at[h, there, rows_at(p), :],
            c_sem.at[k, p], cr_sem.at[h, there, p],
            place(ends * beside + (1 - ends) * there, mid, core),
        )

    def line_wait(source, there, p):
        remote(
            cs.at[0, rows_at(p), :], cr.at[source, there, rows_at(p), :],
            c_sem.at[0, p], cr_sem.at[source, there, p], core_peer,
        ).wait_recv()

    def line_out(k, adds, parts=range(PARTS)):
        there = dest(k)
        for p in parts:
            y_copy(k, p).wait_recv()
            total = po[k, rows_at(p), :] + yr[k, rows_at(p), :].astype(F32)
            if adds:
                line_wait(end_place, there, p)
                total += cr[end_place, there, rows_at(p), :].astype(F32)
            cs[k, rows_at(p), :] = total.astype(BF16)
            line_copy(k, p).start()

    next_to_end = jnp.logical_and(mirrored == 1, inner)

    z_first = remote(z0.at[1 - core], zr.at[0], z_sem.at[0], zr_sem.at[0], core_peer)
    z_across = remote(zs, zr.at[1], z_sem.at[1], zr_sem.at[1], mid_peer)
    z_share = remote(zsum.at[core], zsum.at[core], z_sem.at[2], zr_sem.at[2], core_peer)

    def z_line(source, other):
        return remote(
            zl.at[source], zl.at[source], z_sem.at[3 + other], zr_sem.at[3 + source],
            place(other, mid, core),
        )

    def z_begin():
        low_t = jnp.transpose(low).astype(BF16)
        lanes = jnp.zeros((LANES, width), F32)
        first_row = lax.broadcasted_iota(jnp.int32, (LANES, width), 0) == 0
        for which in range(2):
            for c0 in range(0, cols, piece_cols):
                value = mm(
                    low_t[which * rank : (which + 1) * rank, :],
                    ds[:, which * cols + c0 : which * cols + c0 + piece_cols],
                )
                sbv[which, :, c0 : c0 + piece_cols] = value
                folded = fold_rows(value * value)
                for c1 in range(0, piece_cols, width):
                    lanes += folded[:, c1 : c1 + width]
                    row = smv[which : which + 1, c0 + c1 : c0 + c1 + width]
                    lanes += jnp.where(first_row, row * row, 0.0)
        z_t = mm(bd[...], dt[...])
        z0[0, :rank, :] = z_t[:rank]
        z0[1, :rank, :] = z_t[rank:]
        z0[0, rank:, :] = lanes
        z0[1, rank:, :] = jnp.zeros((LANES, width), F32)
        start(z_first)

    def z_second():
        z_first.wait_recv()
        zs[...] = z0[core] + zr[0]
        start(z_across)

    def z_third():
        z_across.wait_recv()
        zl[h] = zs[...] + zr[1]
        for other in range(nh):
            start(z_line(h, other), h != other)

    def z_fourth():
        for other in range(nh):
            pl.when(h != other)(z_line(other, 0).wait_recv)
        total = zl[0]
        for other in range(1, nh):
            total = total + zl[other]
        zsum[core] = total
        start(z_share)

    def tail():
        remote(
            zsum.at[1 - core], zsum.at[1 - core], z_sem.at[2], zr_sem.at[2], core_peer
        ).wait_recv()
        z_t = jnp.concatenate([zsum[0, :rank, :], zsum[1, :rank, :]], axis=0)
        energies = jnp.sum(z_t * mm_full(z_t, gram[...]), axis=0, keepdims=True)
        energies += jnp.sum(zsum[0, rank:, :] + zsum[1, rank:, :], axis=0, keepdims=True)
        energy = jnp.sum(energies, axis=1, keepdims=True)
        entries = depth * width + 2 * rank * cols * n + 2 * cols * n
        inverse = 1.0 / jnp.sqrt(jnp.maximum(energy, 0.0) / entries + 1e-06)
        for which in range(2):
            sbv[which] = sbv[which] * inverse
        smv[...] = smv[...] * inverse
        put(sbv, step_b)
        put(smv, step_m)
        t_upper, t_lower = split_parts(z_t)
        mine = gat[me]
        sav[...] = jnp.transpose((mm(t_upper, mine) + mm(t_lower, mine)) * inverse)
        put(sav, step_a)
        a_mine = wbuf[pl.ds(pl.multiple_of(me * block, block), block), wide:]
        po[nh - 1] = po[nh - 1] + (mm(a_mine, t_upper) + mm(a_mine, t_lower))

    not_next = jnp.logical_not(next_to_end)

    def line_part(k, p):
        if p >= PARTS:
            return
        if k == 0:
            line_out(0, False, [p])
        else:
            pl.when(not_next)(functools.partial(line_out, k, False, [p]))

    def run(*units):
        for unit in units:
            if callable(unit):
                unit()
            else:
                unit[0](*unit[1:])

    run((q_other, 0), (q_own, 0), (q_second, 0), z_begin, (q_other, 1), z_second)
    run((q_own, 1), (q_second, 1))
    run((p_other, 0), (p_own, 0), (q_other, 2), (p_second, 0), (q_own, 2), (q_second, 2))
    run((p_other, 1), (line_part, 0, 0), (p_own, 1), (line_part, 0, 1), (p_second, 1), z_third)
    run((q_other, 3), (line_part, 0, 2), (q_own, 3), (line_part, 0, 3), (q_second, 3))
    run((p_other, 2), (line_part, 1, 0), (p_own, 2), (line_part, 1, 1), (p_second, 2))
    for k in range(4, nh):
        run((q_other, k), (q_own, k), (q_second, k), (p_other, k - 1), (p_own, k - 1), (p_second, k - 1))
    run((p_other, nh - 1), (line_part, 1, 2), (p_own, nh - 1), (line_part, 1, 3), (p_second, nh - 1))
    run(z_fourth)
    for k in range(2, nh - 1):
        pl.when(next_to_end)(functools.partial(line_out, k - 1, True))
    tail()
    for k in range(2, nh - 1):
        pl.when(not_next)(functools.partial(line_out, k, False))
    pl.when(next_to_end)(functools.partial(line_out, nh - 2, True))
    for p in range(PARTS):
        y_copy(nh - 1, p).wait_recv()
        po[nh - 1, rows_at(p), :] += yr[nh - 1, rows_at(p), :].astype(F32)
    for p in range(PARTS):
        for source in range(nh):
            if source == 0:
                comes = h == 1
            elif source == nh - 1:
                comes = h == nh - 2
            else:
                comes = h != source

            @pl.when(comes)
            def _():
                line_wait(source, h, p)
                po[nh - 1, rows_at(p), :] += cr[source, h, rows_at(p), :].astype(F32)

        gtv[:, p * fine : (p + 1) * fine] = jnp.transpose(po[nh - 1, rows_at(p), :]).astype(BF16)
    put(gtv, gtok)
    for k in range(nh - 1):
        for p in range(PARTS):
            line_copy(k, p).wait_send()
    for when, copy in pending:
        if when is None:
            copy.wait_send()
        else:
            pl.when(when)(copy.wait_send)
    for copy in outs:
        copy.wait()


def hand_on(*refs):
    for source, target in zip(refs[:5], refs[5:]):
        target[...] = source[...]


def per_device(n, tokens, grad_hidden, w_gate, w_up, a_factors, b_factors, magnitudes):
    count, block = tokens.shape
    depth, cols = w_gate.shape
    width = a_factors.shape[1]
    rank = width // 2
    nh = n // 4
    vmem = pl.BlockSpec(memory_space=pltpu.VMEM)
    hbm = pl.BlockSpec(memory_space=pl.ANY)
    dma = pltpu.SemaphoreType.DMA
    outs = (
        jax.ShapeDtypeStruct((count, cols), BF16),
        jax.ShapeDtypeStruct((count, block), BF16),
        jax.ShapeDtypeStruct((block, width), F32),
        jax.ShapeDtypeStruct((2, rank, cols), F32),
        jax.ShapeDtypeStruct((2, cols), F32),
    )
    blocks = pltpu.VMEM((nh, block, count), BF16)
    z_half = (rank + LANES, count)
    results = pl.pallas_call(
        functools.partial(kernel, n),
        out_shape=outs,
        in_specs=[hbm] * 7,
        out_specs=(hbm,) * 5,
        scratch_shapes=[
            pltpu.VMEM((depth, 2 * cols + width), BF16),
            pltpu.VMEM((n, count, block), BF16),
            pltpu.VMEM((count, cols), BF16),
            pltpu.VMEM((width, 2 * cols), BF16),
            pltpu.VMEM((2, cols), F32),
            pltpu.VMEM((8, 2 * cols), F32),
            pltpu.VMEM((width, 2 * cols + width), F32),
            pltpu.VMEM((count, 2 * cols + width), F32),
            pltpu.VMEM((count, count), F32),
            pltpu.VMEM((1, 2 * cols), F32),
            pltpu.VMEM((1, 2 * cols), F32),
            pltpu.VMEM((count, 2 * cols), BF16),
            pltpu.VMEM((2 * cols, count), BF16),
        ]
        + [pltpu.VMEM(o.shape, o.dtype) for o in outs]
        + [
            pltpu.VMEM((block, count), F32),
            blocks, blocks, blocks, blocks, blocks, blocks,
            pltpu.VMEM((nh, block, count), F32),
            blocks,
            pltpu.VMEM((nh, nh, block, count), BF16),
            pltpu.VMEM((2,) + z_half, F32),
            pltpu.VMEM((2,) + z_half, F32),
            pltpu.VMEM(z_half, F32),
            pltpu.VMEM((2,) + z_half, F32),
            pltpu.VMEM((nh,) + z_half, F32),
            dma((3, CHUNKS)),
            dma((5,)),
            dma((5,)),
            dma((24 * nh,)),
            dma((n, 2)),
            dma((nh, PARTS)),
            dma((nh, PARTS)),
            dma((nh, PARTS)),
            dma((nh, PARTS)),
            dma((nh,)),
            dma((nh,)),
            dma((nh, PARTS)),
            dma((nh, nh, PARTS)),
            dma((nh + 3,)),
            dma((nh + 3,)),
        ],
        compiler_params=pltpu.CompilerParams(
            collective_id=0, has_side_effects=True, vmem_limit_bytes=60 * 1024 * 1024
        ),
    )(tokens, grad_hidden, w_gate, w_up, a_factors, b_factors, magnitudes)
    return pl.pallas_call(
        hand_on,
        out_shape=tuple(jax.ShapeDtypeStruct(r.shape, r.dtype) for r in results),
        in_specs=[vmem] * 5,
        out_specs=(vmem,) * 5,
    )(*results)


def solution(mesh):
    in_specs = (
        P("groups", "out"),
        P("groups", "out"),
        P(None, "out"),
        P(None, "out"),
        P(),
        P(None, None, "out"),
        P(None, "out"),
    )
    out_specs = (
        P("groups", "out"),
        P("groups", "out"),
        P(("groups", "out"), None),
        P("groups", None, "out"),
        P("groups", "out"),
    )
    return jax.shard_map(
        functools.partial(per_device, mesh.shape["out"]),
        mesh=mesh, in_specs=in_specs, out_specs=out_specs, check_vma=False,
    )
```
